32 devices in a mesh: depth: 4 (over z), tile: 8 (over y, x, core).
Axes of the slice: x: 2, y: 2, z: 4, core: 2. Of those that a mesh axis runs over, the one named last changes fastest.
Arguments:
- density: bfloat16 [32, 256, 1024], P('depth', None, 'tile'), may hold values from 0 to 1
- view_zoom: float32 [2], replicated, may hold values from 0.5 to 0.9
- view_shift: float32 [2], replicated, may hold values from 0 to 16
- tf_weights: float32 [2, 4, 8], replicated, may hold values from 0.25 to 2
- perm_order: int32 [2, 4], replicated, may hold values from 0 to 3, each once within a row
Outputs:
- image: float32 [2, 4, 256, 1024], P(None, None, 'depth', 'tile')
The draws below stay inside these ranges and needn't reach their ends.
All inputs are finite; a program needn't handle non-finite values.
Results may differ from the reference program's by a relative error of at most 0.0028.
Values may be sent and summed in bfloat16 or wider, within the bound.
A program may use at most 64 MiB of HBM per device.

```python
import jax
import jax.numpy as jnp
from jax import lax

CZ = 8
CX = 128
NY = 256
VIEWS = 2
BASIS = 8
RADIUS = 8
NZ = 32
NX = 1024
N_DEPTH = 4


def spread_matrix(fine_count, coarse_count, spacing):
    fine_pos = jnp.arange(fine_count, dtype=jnp.float32) / spacing
    coarse_pos = jnp.arange(coarse_count, dtype=jnp.float32)
    return jnp.maximum(0.0, 1.0 - jnp.abs(fine_pos[:, None] - coarse_pos[None, :]))


def draw_density(key, part):
    coarse_key = jax.random.fold_in(key, 7101)
    noise_key = jax.random.fold_in(key, 7102)
    depth_coarse = NZ // 4 + 1
    row_coarse = NY // 16 + 1
    width_coarse = NX // 16 + 1
    coarse = jax.random.uniform(coarse_key, (depth_coarse, row_coarse, width_coarse), jnp.float32)
    width_map = spread_matrix(NX, width_coarse, 16.0)
    row_map = spread_matrix(NY, row_coarse, 16.0)
    depth_map = spread_matrix(NZ, depth_coarse, 4.0)
    smooth = jnp.einsum('abc,xc->abx', coarse, width_map, precision=lax.Precision.HIGHEST)
    smooth = jnp.einsum('abx,yb->ayx', smooth, row_map, precision=lax.Precision.HIGHEST)
    smooth = jnp.einsum('ayx,za->zyx', smooth, depth_map, precision=lax.Precision.HIGHEST)
    noise = jax.random.uniform(noise_key, (NZ, NY, NX), jnp.float32)
    column_sign = 1.0 - 2.0 * (jnp.arange(NX, dtype=jnp.int32) % 2).astype(jnp.float32)
    row_sign = 1.0 - 2.0 * (jnp.arange(NY, dtype=jnp.int32) % 2).astype(jnp.float32)
    stripes = 0.15 * (column_sign[None, None, :] + row_sign[None, :, None]) + 0.15
    field = 0.5 * smooth + 0.2 * noise + stripes
    return jnp.clip(field, 0.0, 1.0).astype(jnp.bfloat16)


def setup_inputs(seed: int = 0) -> dict:
    key_list = jax.random.split(jax.random.key(seed), 6)
    density = draw_density(jax.random.fold_in(key_list[5], 71), 0)
    view_zoom = jnp.clip(jax.random.uniform(key_list[1], (VIEWS,), jnp.float32, 0.5, 0.9), 0.5, 0.9)
    view_shift = jnp.clip(jax.random.uniform(key_list[2], (VIEWS,), jnp.float32, 0.0, 16.0), 0.0, 16.0)
    tf_weights = jnp.clip(jax.random.uniform(key_list[3], (VIEWS, 4, BASIS), jnp.float32, 0.25, 2.0), 0.25, 2.0)
    perm_order = jax.vmap(lambda own: jax.random.permutation(own, N_DEPTH))(jax.random.split(key_list[4], VIEWS)).reshape((VIEWS, N_DEPTH)).astype(jnp.int32)
    return {"density": density, "view_zoom": view_zoom, "view_shift": view_shift, "tf_weights": tf_weights, "perm_order": perm_order}


OCCLUSION_GAIN = 1.5
EXTINCTION = 0.5


def blur_weights(radius):
    offsets = jnp.arange(-radius, radius + 1, dtype=jnp.float32)
    tap_weights = jnp.exp(-offsets * offsets / 72.0)
    return tap_weights / jnp.sum(tap_weights)


def occlusion_of(padded, radius, depth_cells, width_cells):
    tap_weights = blur_weights(radius)
    tap_count = 2 * radius + 1
    row_count = padded.shape[1]
    along_depth = tap_weights[0] * padded[0:depth_cells].astype(jnp.float32)
    for tap_index in range(1, tap_count):
        along_depth = along_depth + tap_weights[tap_index] * padded[tap_index:tap_index + depth_cells].astype(jnp.float32)
    padded_rows = jnp.pad(along_depth, ((0, 0), (radius, radius), (0, 0)))
    along_rows = tap_weights[0] * padded_rows[:, 0:row_count]
    for tap_index in range(1, tap_count):
        along_rows = along_rows + tap_weights[tap_index] * padded_rows[:, tap_index:tap_index + row_count]
    along_width = tap_weights[0] * along_rows[:, :, 0:width_cells]
    for tap_index in range(1, tap_count):
        along_width = along_width + tap_weights[tap_index] * along_rows[:, :, tap_index:tap_index + width_cells]
    return jnp.exp(-OCCLUSION_GAIN * along_width).astype(jnp.bfloat16)


def resample_table(view_zoom, view_shift, row_count):
    pixel_pos = jnp.arange(row_count, dtype=jnp.float32)
    where_at = view_zoom[:, None] * pixel_pos[None, :] + view_shift[:, None]
    cell_pos = jnp.arange(row_count, dtype=jnp.float32)
    interp_table = jnp.maximum(0.0, 1.0 - jnp.abs(where_at[:, :, None] - cell_pos[None, None, :]))
    return interp_table.reshape(-1, row_count).astype(jnp.bfloat16)


def render_slab(slab_density, slab_shade, interp_table, tf_weights, depth_total):
    view_count = tf_weights.shape[0]
    basis_count = tf_weights.shape[2]
    row_count = slab_density.shape[1]
    width_cells = slab_density.shape[2]

    def one_slice(state_pair, cell_pair):
        colour, passing = state_pair
        density_rows, shade_rows = cell_pair
        stacked = jnp.concatenate([density_rows, shade_rows], axis=1)
        sampled = jnp.dot(interp_table, stacked, preferred_element_type=jnp.float32)
        sampled = sampled.reshape(view_count, row_count, 2 * width_cells)
        sampled_density = sampled[:, :, :width_cells]
        sampled_shade = sampled[:, :, width_cells:]
        values = jnp.zeros((view_count, 4, row_count, width_cells), jnp.float32)
        for basis_index in range(basis_count):
            offset = sampled_density * (basis_count - 1) - basis_index
            bump_value = jnp.exp(-0.5 * offset * offset)
            values = values + tf_weights[:, :, basis_index][:, :, None, None] * bump_value[:, None]
        opacity = 1.0 - jnp.exp(-(EXTINCTION / depth_total) * values[:, 3])
        lit_part = sampled_shade * opacity
        emitted = jnp.concatenate([values[:, 0:3] * lit_part[:, None], opacity[:, None]], axis=1)
        colour = colour + passing[:, None] * emitted
        passing = passing * (1.0 - opacity)
        return (colour, passing), None

    initial = (jnp.zeros((view_count, 4, row_count, width_cells), jnp.float32),
               jnp.ones((view_count, row_count, width_cells), jnp.float32))
    final_state, _ = lax.scan(one_slice, initial, (slab_density, slab_shade))
    return final_state[0].astype(jnp.bfloat16)


def composite(slab_stack, perm_order):
    slab_count = slab_stack.shape[0]
    view_count = slab_stack.shape[1]
    pictures = []
    for view_index in range(view_count):
        per_view = slab_stack[:, view_index]

        def place(state_pair, position):
            picture, passing = state_pair
            chosen = perm_order[view_index, position].astype(jnp.int32)
            slab_now = lax.dynamic_index_in_dim(per_view, chosen, 0, keepdims=False).astype(jnp.float32)
            picture = picture + passing[None] * slab_now
            passing = passing * (1.0 - slab_now[3])
            return (picture, passing), None

        initial = (jnp.zeros(per_view.shape[1:], jnp.float32), jnp.ones(per_view.shape[2:], jnp.float32))
        final_state, _ = lax.scan(place, initial, jnp.arange(slab_count, dtype=jnp.int32))
        pictures.append(final_state[0])
    return jnp.stack(pictures)


def reference(density, view_zoom, view_shift, tf_weights, perm_order):
    slab_count = NZ // CZ
    interp_table = resample_table(view_zoom, view_shift, NY)
    padded = jnp.pad(density, ((RADIUS, RADIUS), (0, 0), (RADIUS, RADIUS)))

    def render_pair(cell_pair):
        return render_slab(cell_pair[0], cell_pair[1], interp_table, tf_weights, NZ)

    def one_tile(tile_index):
        first_column = (tile_index * CX).astype(jnp.int32)
        region = lax.dynamic_slice_in_dim(padded, first_column, CX + 2 * RADIUS, 2)
        shade = occlusion_of(region, RADIUS, NZ, CX)
        tile_density = lax.dynamic_slice_in_dim(density, first_column, CX, 2)
        slab_stack = lax.map(render_pair, (tile_density.reshape(slab_count, CZ, NY, CX),
                                           shade.reshape(slab_count, CZ, NY, CX)))
        return composite(slab_stack, perm_order)

    tile_images = lax.map(one_tile, jnp.arange(NX // CX, dtype=jnp.int32))
    return jnp.transpose(tile_images, (1, 2, 3, 0, 4)).reshape(VIEWS, 4, NY, NX)
```

```python
import functools
import math

import jax
import jax.numpy as jnp
import numpy as np
from jax import lax
from jax.experimental import pallas as pl
from jax.experimental.pallas import tpu as pltpu
from jax.sharding import PartitionSpec as P

RADIUS = 8
OCCLUSION_GAIN = 1.5
EXTINCTION = 0.5
LOG2E = math.log2(math.e)
GROUP = 16
CHUNK = 32


def rounded_taps():
    offsets = np.arange(-RADIUS, RADIUS + 1, dtype=np.float64)
    taps = np.exp(-offsets * offsets / 72.0)
    taps = (taps / taps.sum()).astype(jnp.bfloat16).astype(np.float64)
    return taps, float(taps.sum())


def band(out_count, in_count, shift, taps):
    offset = np.arange(in_count)[None, :] + shift - np.arange(out_count)[:, None]
    inside = np.abs(offset) <= RADIUS
    return np.where(inside, taps[np.clip(offset + RADIUS, 0, 2 * RADIUS)], 0.0)


def constants(cells, rows, width):
    taps, total = rounded_taps()
    pack = np.zeros((cells, width, width), np.float32)
    low = np.zeros((width, cells, width))
    high = np.zeros((width, cells, width))
    half = cells * RADIUS
    from_low = band(width, RADIUS, -RADIUS, taps).T
    from_high = band(width, RADIUS, width, taps).T
    for z in range(cells):
        for j in range(RADIUS):
            pack[z, j, z * RADIUS + j] = 1.0
            pack[z, width - RADIUS + j, half + z * RADIUS + j] = 1.0
        low[half + z * RADIUS : half + (z + 1) * RADIUS, z] = from_low
        high[z * RADIUS : (z + 1) * RADIUS, z] = from_high
    halo = np.concatenate([low, high]).reshape(2 * width, cells * width)
    depth = np.kron(band(cells, 3 * cells, -cells, taps), np.eye(GROUP))
    arrays = (
        pack.reshape(cells * width, width),
        band(width, width, 0, taps).T,
        halo,
        band(rows, rows, 0, taps),
        depth,
    )
    return [jnp.asarray(a.astype(jnp.bfloat16)) for a in arrays], total


def matmul(a, b):
    return jnp.dot(a, b, preferred_element_type=jnp.float32)


def kernel(
    slabs, tiles, tap_total,
    density, zoom, shift, weights, order, pack_m, width_m, halo_m, height_m, depth_m,
    image,
    table, packed, from_left, from_right, plane, from_low, from_high, sampled, lit, shade, slab, *rest,
):
    views, channels, basis = weights.shape
    cells, rows, width = density.shape
    recv = rest[:views]
    tile_send, tile_recv, depth_send, depth_recv, slab_send, slab_recv = rest[views:]
    group_rows = rows // slabs
    d = lax.axis_index("depth")
    t = lax.axis_index("tile")
    bf16 = jnp.bfloat16

    barrier = pltpu.get_barrier_semaphore()

    def greet(peer):
        pl.semaphore_signal(barrier, inc=1, device_id=peer, device_id_type=pl.DeviceIdType.MESH)

    for j in range(slabs):
        @pl.when(j != d)
        def _():
            greet({"depth": j})

    @pl.when(t > 0)
    def _():
        greet({"tile": t - 1})

    @pl.when(t < tiles - 1)
    def _():
        greet({"tile": t + 1})

    def remote(src, dst, send, recv_sem, peer):
        return pltpu.make_async_remote_copy(
            src_ref=src, dst_ref=dst, send_sem=send, recv_sem=recv_sem,
            device_id=peer, device_id_type=pl.DeviceIdType.MESH,
        )

    whole = jnp.concatenate([density[z] for z in range(cells)], axis=1)
    packed[...] = matmul(whole, pack_m[...]).astype(bf16)
    to_left = remote(packed, from_right, tile_send.at[0], tile_recv.at[1], {"tile": t - 1})
    to_right = remote(packed, from_left, tile_send.at[1], tile_recv.at[0], {"tile": t + 1})

    pl.semaphore_wait(
        barrier, slabs - 1 + (t > 0).astype(jnp.int32) + (t < tiles - 1).astype(jnp.int32)
    )

    @pl.when(t > 0)
    def _():
        to_left.start()

    @pl.when(t < tiles - 1)
    def _():
        to_right.start()

    @pl.when(t == 0)
    def _():
        from_left[...] = jnp.zeros_like(from_left)

    @pl.when(t == tiles - 1)
    def _():
        from_right[...] = jnp.zeros_like(from_right)

    @pl.when(d == 0)
    def _():
        from_low[...] = jnp.zeros_like(from_low)

    @pl.when(d == slabs - 1)
    def _():
        from_high[...] = jnp.zeros_like(from_high)

    pixel = lax.broadcasted_iota(jnp.int32, (rows, rows), 0).astype(jnp.float32)
    cell = lax.broadcasted_iota(jnp.int32, (rows, rows), 1).astype(jnp.float32)
    for v in range(views):
        where_at = zoom[v] * pixel + shift[v]
        table[v * rows : (v + 1) * rows] = jnp.maximum(0.0, 1.0 - jnp.abs(where_at - cell)).astype(bf16)

    def resample(source):
        for z in range(0, cells, 2):
            pair = matmul(table[...], jnp.concatenate([source[z], source[z + 1]], axis=1))
            sampled[z] = pair[:, :width]
            sampled[z + 1] = pair[:, width:]

    resample(density)
    inner = matmul(density[...].reshape(cells * rows, width), width_m[...])

    @pl.when(t > 0)
    def _():
        to_left.wait_send()
        to_right.wait_recv()

    @pl.when(t < tiles - 1)
    def _():
        to_right.wait_send()
        to_left.wait_recv()

    outer = matmul(jnp.concatenate([from_left[...], from_right[...]], axis=1), halo_m[...])
    along_width = jnp.concatenate(
        [inner[z * rows : (z + 1) * rows] + outer[:, z * width : (z + 1) * width] for z in range(cells)],
        axis=1,
    ).astype(bf16)
    flat = matmul(height_m[...], along_width).astype(bf16)
    for z in range(cells):
        plane[z] = flat[:, z * width : (z + 1) * width]

    to_below = remote(plane, from_high, depth_send.at[0], depth_recv.at[1], {"depth": d - 1})
    to_above = remote(plane, from_low, depth_send.at[1], depth_recv.at[0], {"depth": d + 1})

    @pl.when(d > 0)
    def _():
        to_below.start()

    @pl.when(d < slabs - 1)
    def _():
        to_above.start()

    chunk = min(CHUNK, group_rows)
    per_group = group_rows // chunk
    extinction = -(EXTINCTION / (cells * slabs)) * LOG2E
    peak = basis - 1
    for v in range(views):
        coef = [
            [
                weights[v, c, k] * (math.exp(-0.5 * k * k) * (extinction if c == channels - 1 else 1.0))
                for k in range(basis)
            ]
            for c in range(channels)
        ]

        def transfer(i, carry, v=v, coef=coef):
            first = pl.multiple_of(i * chunk, chunk)
            passing = jnp.ones((chunk, width), jnp.float32)
            for z in range(cells):
                s = sampled[z, pl.ds(v * rows + first, chunk), :]
                fall = jnp.exp2((-0.5 * peak * peak * LOG2E) * (s * s))
                ratio = jnp.exp2((peak * LOG2E) * s)
                sums = []
                for c in range(channels):
                    total = coef[c][basis - 1] * ratio + coef[c][basis - 2]
                    for k in range(basis - 3, -1, -1):
                        total = total * ratio + coef[c][k]
                    sums.append(total)
                later = passing * jnp.exp2(fall * sums[-1])
                share = (passing - later) * fall
                for c in range(channels - 1):
                    lit[v, c, z, pl.ds(first, chunk), :] = share * sums[c]
                passing = later
            group = i // per_group
            inside = pl.multiple_of((i % per_group) * chunk, chunk)
            slab[v, group, channels - 1, pl.ds(inside, chunk), :] = (1.0 - passing).astype(bf16)
            return carry

        lax.fori_loop(0, rows // chunk, transfer, 0)

    @pl.when(d > 0)
    def _():
        to_below.wait_send()
        to_above.wait_recv()

    @pl.when(d < slabs - 1)
    def _():
        to_above.wait_send()
        to_below.wait_recv()

    gain = -OCCLUSION_GAIN * LOG2E / tap_total**3
    for g in range(0, rows, 2 * GROUP):
        def column(at):
            part = pl.ds(at, GROUP)
            return jnp.concatenate(
                [ref[:, part, :].reshape(cells * GROUP, width) for ref in (from_low, plane, from_high)], axis=0
            )

        both = matmul(depth_m[...], jnp.concatenate([column(g), column(g + GROUP)], axis=1))
        both = jnp.exp2(gain * both).astype(bf16)
        shade[:, g : g + GROUP, :] = both[:, :width].reshape(cells, GROUP, width)
        shade[:, g + GROUP : g + 2 * GROUP, :] = both[:, width:].reshape(cells, GROUP, width)
    resample(shade)

    def slab_copy(v, j):
        return remote(slab.at[v, j], recv[v].at[d], slab_send.at[v, j], slab_recv.at[v, d], {"depth": j})

    for v in range(views):
        for j in range(slabs):
            for i in range(per_group):
                here = slice(i * chunk, (i + 1) * chunk)
                at = slice(j * group_rows + i * chunk, j * group_rows + (i + 1) * chunk)
                colour = [jnp.zeros((chunk, width), jnp.float32)] * (channels - 1)
                for z in range(cells):
                    s = sampled[z, v * rows + at.start : v * rows + at.stop, :]
                    colour = [colour[c] + lit[v, c, z, at, :] * s for c in range(channels - 1)]
                for c in range(channels - 1):
                    slab[v, j, c, here, :] = colour[c].astype(bf16)

            @pl.when(j != d)
            def _():
                slab_copy(v, j).start()

            @pl.when(j == d)
            def _():
                recv[v][d] = slab[v, j]

    for v in range(views):
        for j in range(slabs):
            @pl.when(j != d)
            def _():
                slab_copy(v, j).wait_send()
                remote(slab.at[v, j], recv[v].at[j], slab_send.at[v, j], slab_recv.at[v, j], {"depth": j}).wait_recv()

        picture = jnp.zeros((channels, group_rows, width), jnp.float32)
        passing = jnp.ones((group_rows, width), jnp.float32)
        for q in range(slabs):
            layer = recv[v][order[v, q]].astype(jnp.float32)
            picture = picture + passing[None] * layer
            passing = passing * (1.0 - layer[channels - 1])
        image[v] = picture


def local(slabs, tiles, density, view_zoom, view_shift, tf_weights, perm_order):
    cells, rows, width = density.shape
    views, channels, _ = tf_weights.shape
    group_rows = rows // slabs
    matrices, tap_total = constants(cells, rows, width)
    vmem = pl.BlockSpec(memory_space=pltpu.VMEM)
    smem = pl.BlockSpec(memory_space=pltpu.SMEM)
    bf16 = jnp.bfloat16
    block = pltpu.VMEM((cells, rows, width), bf16)
    edge = pltpu.VMEM((rows, width), bf16)
    dma = pltpu.SemaphoreType.DMA
    return pl.pallas_call(
        functools.partial(kernel, slabs, tiles, tap_total),
        out_shape=jax.ShapeDtypeStruct((views, channels, group_rows, width), jnp.float32),
        in_specs=[vmem, smem, smem, smem, smem] + [vmem] * len(matrices),
        out_specs=vmem,
        scratch_shapes=[
            pltpu.VMEM((views * rows, rows), bf16),
            edge, edge, edge,
            block, block, block,
            pltpu.VMEM((cells, views * rows, width), jnp.float32),
            pltpu.VMEM((views, channels - 1, cells, rows, width), jnp.float32),
            block,
            pltpu.VMEM((views, slabs, channels, group_rows, width), bf16),
        ]
        + [pltpu.VMEM((slabs, channels, group_rows, width), bf16)] * views
        + [dma((2,)), dma((2,)), dma((2,)), dma((2,)), dma((views, slabs)), dma((views, slabs))],
        compiler_params=pltpu.CompilerParams(
            collective_id=0, has_side_effects=True, vmem_limit_bytes=60 * 1024 * 1024
        ),
    )(density, view_zoom, view_shift, tf_weights, perm_order, *matrices)


def solution(mesh):
    placed = (P("depth", None, "tile"), P(), P(), P(), P())
    return jax.shard_map(
        functools.partial(local, mesh.shape["depth"], mesh.shape["tile"]),
        mesh=mesh, in_specs=placed, out_specs=P(None, None, "depth", "tile"), check_vma=False,
    )
```

```python
import functools
import math

import jax
import jax.numpy as jnp
import numpy as np
from jax import lax
from jax.experimental import pallas as pl
from jax.experimental.pallas import tpu as pltpu
from jax.sharding import PartitionSpec as P

RADIUS = 8
OCCLUSION_GAIN = 1.5
EXTINCTION = 0.5
MAX_ZOOM = 0.9
MAX_SHIFT = 16.0
LOG2E = math.log2(math.e)
GROUP = 16
CHUNK = 32


def rounded_taps():
    offsets = np.arange(-RADIUS, RADIUS + 1, dtype=np.float64)
    taps = np.exp(-offsets * offsets / 72.0)
    taps = (taps / taps.sum()).astype(jnp.bfloat16).astype(np.float64)
    return taps, float(taps.sum())


def band(out_count, in_count, shift, taps):
    offset = np.arange(in_count)[None, :] + shift - np.arange(out_count)[:, None]
    inside = np.abs(offset) <= RADIUS
    return np.where(inside, taps[np.clip(offset + RADIUS, 0, 2 * RADIUS)], 0.0)


def constants(cells, rows, width):
    taps, total = rounded_taps()
    pack = np.zeros((cells, width, width), np.float32)
    low = np.zeros((width, cells, width))
    high = np.zeros((width, cells, width))
    half = cells * RADIUS
    from_low = band(width, RADIUS, -RADIUS, taps).T
    from_high = band(width, RADIUS, width, taps).T
    for z in range(cells):
        for j in range(RADIUS):
            pack[z, j, z * RADIUS + j] = 1.0
            pack[z, width - RADIUS + j, half + z * RADIUS + j] = 1.0
        low[half + z * RADIUS : half + (z + 1) * RADIUS, z] = from_low
        high[z * RADIUS : (z + 1) * RADIUS, z] = from_high
    halo = np.concatenate([low, high]).reshape(2 * width, cells * width)
    depth = np.kron(band(cells, 3 * cells, -cells, taps), np.eye(GROUP))
    arrays = (
        pack.reshape(cells * width, width),
        band(width, width, 0, taps).T,
        halo,
        band(rows, rows, 0, taps),
        depth,
    )
    return [jnp.asarray(a.astype(jnp.bfloat16)) for a in arrays], total


def matmul(a, b):
    return jnp.dot(a, b, preferred_element_type=jnp.float32)


def kernel(
    slabs, tiles, tap_total,
    density_in, zoom, shift, weights, order, pack_in, width_in, halo_in, height_in, depth_in,
    image,
    density, pack_m, width_m, halo_m, height_m, depth_m,
    table, packed, from_left, from_right, plane, from_low, from_high, sampled, lit, shade, alpha, slab, recv_alpha, *rest,
):
    views, channels, basis = weights.shape
    cells, rows, width = density_in.shape
    used = used_rows(rows)
    recv = rest[:views]
    fetch_sem, tile_send, tile_recv, depth_send, depth_recv, alpha_send, alpha_recv, slab_send, slab_recv = rest[views:]
    group_rows = rows // slabs
    d = lax.axis_index("depth")
    t = lax.axis_index("tile")
    bf16 = jnp.bfloat16

    barrier = pltpu.get_barrier_semaphore()

    def greet(peer):
        pl.semaphore_signal(barrier, inc=1, device_id=peer, device_id_type=pl.DeviceIdType.MESH)

    for j in range(slabs):
        @pl.when(j != d)
        def _():
            greet({"depth": j})

    @pl.when(t > 0)
    def _():
        greet({"tile": t - 1})

    @pl.when(t < tiles - 1)
    def _():
        greet({"tile": t + 1})

    sources = (density_in, pack_in, width_in, halo_in, height_in, depth_in)
    places = (density, pack_m, width_m, halo_m, height_m, depth_m)
    fetches = [
        pltpu.make_async_copy(src, dst, fetch_sem.at[i]) for i, (src, dst) in enumerate(zip(sources, places))
    ]
    for fetch in fetches:
        fetch.start()
    fetches[0].wait()
    fetches[1].wait()

    def remote(src, dst, send, recv_sem, peer):
        return pltpu.make_async_remote_copy(
            src_ref=src, dst_ref=dst, send_sem=send, recv_sem=recv_sem,
            device_id=peer, device_id_type=pl.DeviceIdType.MESH,
        )

    whole = jnp.concatenate([density[z] for z in range(cells)], axis=1)
    packed[...] = matmul(whole, pack_m[...]).astype(bf16)
    to_left = remote(packed, from_right, tile_send.at[0], tile_recv.at[1], {"tile": t - 1})
    to_right = remote(packed, from_left, tile_send.at[1], tile_recv.at[0], {"tile": t + 1})

    pl.semaphore_wait(
        barrier, slabs - 1 + (t > 0).astype(jnp.int32) + (t < tiles - 1).astype(jnp.int32)
    )

    @pl.when(t > 0)
    def _():
        to_left.start()

    @pl.when(t < tiles - 1)
    def _():
        to_right.start()

    @pl.when(t == 0)
    def _():
        from_left[...] = jnp.zeros_like(from_left)

    @pl.when(t == tiles - 1)
    def _():
        from_right[...] = jnp.zeros_like(from_right)

    if used < rows:
        from_low[:, used:] = jnp.zeros((cells, rows - used, width), bf16)
        from_high[:, used:] = jnp.zeros((cells, rows - used, width), bf16)

    @pl.when(d == 0)
    def _():
        from_low[...] = jnp.zeros_like(from_low)

    @pl.when(d == slabs - 1)
    def _():
        from_high[...] = jnp.zeros_like(from_high)

    pixel = lax.broadcasted_iota(jnp.int32, (rows, rows), 0).astype(jnp.float32)
    cell = lax.broadcasted_iota(jnp.int32, (rows, rows), 1).astype(jnp.float32)
    for v in range(views):
        where_at = zoom[v] * pixel + shift[v]
        table[v * rows : (v + 1) * rows] = jnp.maximum(0.0, 1.0 - jnp.abs(where_at - cell)).astype(bf16)

    def resample(source):
        for z in range(0, cells, 2):
            pair = matmul(table[...], jnp.concatenate([source[z], source[z + 1]], axis=1))
            sampled[z] = pair[:, :width]
            sampled[z + 1] = pair[:, width:]

    resample(density)
    for fetch in fetches[2:]:
        fetch.wait()
    inner = matmul(density[...].reshape(cells * rows, width), width_m[...])

    @pl.when(t > 0)
    def _():
        to_left.wait_send()
        to_right.wait_recv()

    @pl.when(t < tiles - 1)
    def _():
        to_right.wait_send()
        to_left.wait_recv()

    outer = matmul(jnp.concatenate([from_left[...], from_right[...]], axis=1), halo_m[...])
    along_width = jnp.concatenate(
        [inner[z * rows : (z + 1) * rows] + outer[:, z * width : (z + 1) * width] for z in range(cells)],
        axis=1,
    ).astype(bf16)
    flat = matmul(height_m[...], along_width).astype(bf16)
    for z in range(cells):
        plane[z] = flat[:, z * width : (z + 1) * width]

    to_below = remote(plane.at[:, :used], from_high.at[:, :used], depth_send.at[0], depth_recv.at[1], {"depth": d - 1})
    to_above = remote(plane.at[:, :used], from_low.at[:, :used], depth_send.at[1], depth_recv.at[0], {"depth": d + 1})

    @pl.when(d > 0)
    def _():
        to_below.start()

    @pl.when(d < slabs - 1)
    def _():
        to_above.start()

    chunk = min(CHUNK, group_rows)
    per_group = group_rows // chunk
    extinction = -(EXTINCTION / (cells * slabs)) * LOG2E
    peak = basis - 1
    for v in range(views):
        coef = [
            [
                weights[v, c, k] * (math.exp(-0.5 * k * k) * (extinction if c == channels - 1 else 1.0))
                for k in range(basis)
            ]
            for c in range(channels)
        ]

        def transfer(i, carry, v=v, coef=coef):
            first = pl.multiple_of(i * chunk, chunk)
            passing = jnp.ones((chunk, width), jnp.float32)
            for z in range(cells):
                s = sampled[z, pl.ds(v * rows + first, chunk), :]
                fall = jnp.exp2((-0.5 * peak * peak * LOG2E) * (s * s))
                ratio = jnp.exp2((peak * LOG2E) * s)
                sums = []
                for c in range(channels):
                    total = coef[c][basis - 1] * ratio + coef[c][basis - 2]
                    for k in range(basis - 3, -1, -1):
                        total = total * ratio + coef[c][k]
                    sums.append(total)
                later = passing * jnp.exp2(fall * sums[-1])
                share = (passing - later) * fall
                for c in range(channels - 1):
                    lit[v, c, z, pl.ds(first, chunk), :] = share * sums[c]
                passing = later
            group = i // per_group
            inside = pl.multiple_of((i % per_group) * chunk, chunk)
            alpha[group, v, pl.ds(inside, chunk), :] = (1.0 - passing).astype(bf16)
            return carry

        lax.fori_loop(0, rows // chunk, transfer, 0)

    @pl.when(d > 0)
    def _():
        to_below.wait_send()
        to_above.wait_recv()

    @pl.when(d < slabs - 1)
    def _():
        to_above.wait_send()
        to_below.wait_recv()

    def peer_of(k):
        return lax.rem(d + k, slabs)

    def alpha_copy(k):
        return remote(alpha.at[peer_of(k)], recv_alpha.at[d], alpha_send.at[k], alpha_recv.at[d], {"depth": peer_of(k)})

    others = sorted(range(1, slabs), key=lambda k: abs(2 * k - slabs))
    for k in others:
        alpha_copy(k).start()
    recv_alpha[d] = alpha[d]

    gain = -OCCLUSION_GAIN * LOG2E / tap_total**3
    for g in range(0, rows, 2 * GROUP):
        def column(at):
            part = pl.ds(at, GROUP)
            return jnp.concatenate(
                [ref[:, part, :].reshape(cells * GROUP, width) for ref in (from_low, plane, from_high)], axis=0
            )

        both = matmul(depth_m[...], jnp.concatenate([column(g), column(g + GROUP)], axis=1))
        both = jnp.exp2(gain * both).astype(bf16)
        shade[:, g : g + GROUP, :] = both[:, :width].reshape(cells, GROUP, width)
        shade[:, g + GROUP : g + 2 * GROUP, :] = both[:, width:].reshape(cells, GROUP, width)
    resample(shade)

    def slab_copy(v, k):
        return remote(
            slab.at[v, k], recv[v].at[d], slab_send.at[v, k], slab_recv.at[v, d], {"depth": peer_of(k)}
        )

    for v in range(views):
        for k in others + [0]:
            start = pl.multiple_of(peer_of(k) * group_rows, group_rows)
            for i in range(per_group):
                colour = [jnp.zeros((chunk, width), jnp.float32)] * (channels - 1)
                for z in range(cells):
                    s = sampled[z, pl.ds(v * rows + start + i * chunk, chunk), :]
                    colour = [
                        colour[c] + lit[v, c, z, pl.ds(start + i * chunk, chunk), :] * s
                        for c in range(channels - 1)
                    ]
                for c in range(channels - 1):
                    tint = colour[c].astype(bf16)
                    if k:
                        slab[v, k, c, i * chunk : (i + 1) * chunk, :] = tint
                    else:
                        recv[v][d, c, i * chunk : (i + 1) * chunk, :] = tint
            if k:
                slab_copy(v, k).start()

    for k in others:
        peer = peer_of(k)
        alpha_copy(k).wait_send()
        remote(
            alpha.at[peer], recv_alpha.at[peer], alpha_send.at[k], alpha_recv.at[peer], {"depth": peer}
        ).wait_recv()
    for v in range(views):
        for k in others:
            peer = peer_of(k)
            slab_copy(v, k).wait_send()
            remote(
                slab.at[v, k], recv[v].at[peer], slab_send.at[v, k], slab_recv.at[v, peer], {"depth": peer}
            ).wait_recv()

        picture = jnp.zeros((channels - 1, group_rows, width), jnp.float32)
        cover = jnp.zeros((group_rows, width), jnp.float32)
        passing = jnp.ones((group_rows, width), jnp.float32)
        for q in range(slabs):
            slot = order[v, q]
            dense = recv_alpha[slot, v].astype(jnp.float32)
            picture = picture + passing[None] * recv[v][slot].astype(jnp.float32)
            cover = cover + passing * dense
            passing = passing * (1.0 - dense)
        image[v, : channels - 1] = picture
        image[v, channels - 1] = cover


def used_rows(rows):
    last = math.floor(MAX_ZOOM * (rows - 1) + MAX_SHIFT) + 1
    return min(rows, -(-(last + 1) // 8) * 8)


def local(slabs, tiles, density, view_zoom, view_shift, tf_weights, perm_order):
    cells, rows, width = density.shape
    views, channels, _ = tf_weights.shape
    group_rows = rows // slabs
    matrices, tap_total = constants(cells, rows, width)
    vmem = pl.BlockSpec(memory_space=pltpu.VMEM)
    hbm = pl.BlockSpec(memory_space=pl.ANY)
    smem = pl.BlockSpec(memory_space=pltpu.SMEM)
    bf16 = jnp.bfloat16
    block = pltpu.VMEM((cells, rows, width), bf16)
    edge = pltpu.VMEM((rows, width), bf16)
    dma = pltpu.SemaphoreType.DMA
    return pl.pallas_call(
        functools.partial(kernel, slabs, tiles, tap_total),
        out_shape=jax.ShapeDtypeStruct((views, channels, group_rows, width), jnp.float32),
        in_specs=[hbm, smem, smem, smem, smem] + [hbm] * len(matrices),
        out_specs=vmem,
        scratch_shapes=[block]
        + [pltpu.VMEM(m.shape, bf16) for m in matrices]
        + [
            pltpu.VMEM((views * rows, rows), bf16),
            edge, edge, edge,
            block, block, block,
            pltpu.VMEM((cells, views * rows, width), jnp.float32),
            pltpu.VMEM((views, channels - 1, cells, rows, width), jnp.float32),
            block,
            pltpu.VMEM((slabs, views, group_rows, width), bf16),
            pltpu.VMEM((views, slabs, channels - 1, group_rows, width), bf16),
            pltpu.VMEM((slabs, views, group_rows, width), bf16),
        ]
        + [pltpu.VMEM((slabs, channels - 1, group_rows, width), bf16)] * views
        + [dma((1 + len(matrices),)), dma((2,)), dma((2,)), dma((2,)), dma((2,)), dma((slabs,)), dma((slabs,))]
        + [dma((views, slabs)), dma((views, slabs))],
        compiler_params=pltpu.CompilerParams(
            collective_id=0, has_side_effects=True, vmem_limit_bytes=60 * 1024 * 1024
        ),
    )(density, view_zoom, view_shift, tf_weights, perm_order, *matrices)


def solution(mesh):
    placed = (P("depth", None, "tile"), P(), P(), P(), P())
    return jax.shard_map(
        functools.partial(local, mesh.shape["depth"], mesh.shape["tile"]),
        mesh=mesh, in_specs=placed, out_specs=P(None, None, "depth", "tile"), check_vma=False,
    )
```

```python
import functools
import math

import jax
import jax.numpy as jnp
import numpy as np
from jax import lax
from jax.experimental import pallas as pl
from jax.experimental.pallas import tpu as pltpu
from jax.sharding import PartitionSpec as P

RADIUS = 8
OCCLUSION_GAIN = 1.5
EXTINCTION = 0.5
LOG2E = math.log2(math.e)
GROUP = 16
CHUNK = 32


def rounded_taps():
    offsets = np.arange(-RADIUS, RADIUS + 1, dtype=np.float64)
    taps = np.exp(-offsets * offsets / 72.0)
    taps = (taps / taps.sum()).astype(jnp.bfloat16).astype(np.float64)
    return taps, float(taps.sum())


def band(out_count, in_count, shift, taps):
    offset = np.arange(in_count)[None, :] + shift - np.arange(out_count)[:, None]
    inside = np.abs(offset) <= RADIUS
    return np.where(inside, taps[np.clip(offset + RADIUS, 0, 2 * RADIUS)], 0.0)


def constants(cells, rows, width):
    taps, total = rounded_taps()
    pack = np.zeros((cells, width, width), np.float32)
    low = np.zeros((width, cells, width))
    high = np.zeros((width, cells, width))
    half = cells * RADIUS
    from_low = band(width, RADIUS, -RADIUS, taps).T
    from_high = band(width, RADIUS, width, taps).T
    for z in range(cells):
        for j in range(RADIUS):
            pack[z, j, z * RADIUS + j] = 1.0
            pack[z, width - RADIUS + j, half + z * RADIUS + j] = 1.0
        low[half + z * RADIUS : half + (z + 1) * RADIUS, z] = from_low
        high[z * RADIUS : (z + 1) * RADIUS, z] = from_high
    halo = (low + high).reshape(width, cells * width)
    depth = np.kron(band(cells, 3 * cells, -cells, taps), np.eye(GROUP))
    arrays = (
        pack.reshape(cells * width, width),
        band(width, width, 0, taps).T,
        halo,
        band(rows, rows, 0, taps),
        depth,
    )
    return [jnp.asarray(a.astype(jnp.bfloat16)) for a in arrays], total


def matmul(a, b):
    return jnp.dot(a, b, preferred_element_type=jnp.float32)


def kernel(
    slabs, tiles, tap_total,
    density_in, zoom, shift, weights, order, pack_in, width_in, halo_in, height_in, depth_in,
    image,
    density, pack_m, width_m, halo_m, height_m, depth_m,
    table, packed, from_left, from_right, edges, edges_low, edges_high,
    plane, plane_low, plane_high, from_low, from_high, sampled, lit, shade, alpha, slab, recv_alpha, *rest,
):
    views, channels, basis = weights.shape
    cells, rows, width = density_in.shape
    recv = rest[:views]
    fetch_sem, tile_send, tile_recv, depth_send, depth_recv, edge_send, edge_recv, alpha_send, alpha_recv, slab_send, slab_recv = rest[views:]
    group_rows = rows // slabs
    d = lax.axis_index("depth")
    t = lax.axis_index("tile")
    bf16 = jnp.bfloat16

    barrier = pltpu.get_barrier_semaphore()

    def greet(peer):
        pl.semaphore_signal(barrier, inc=1, device_id=peer, device_id_type=pl.DeviceIdType.MESH)

    for j in range(slabs):
        @pl.when(j != d)
        def _():
            greet({"depth": j})

    @pl.when(t > 0)
    def _():
        greet({"tile": t - 1})

    @pl.when(t < tiles - 1)
    def _():
        greet({"tile": t + 1})

    sources = (density_in, pack_in, width_in, halo_in, height_in, depth_in)
    places = (density, pack_m, width_m, halo_m, height_m, depth_m)
    fetches = [
        pltpu.make_async_copy(src, dst, fetch_sem.at[i]) for i, (src, dst) in enumerate(zip(sources, places))
    ]
    for fetch in fetches:
        fetch.start()
    fetches[0].wait()
    fetches[1].wait()

    def remote(src, dst, send, recv_sem, peer):
        return pltpu.make_async_remote_copy(
            src_ref=src, dst_ref=dst, send_sem=send, recv_sem=recv_sem,
            device_id=peer, device_id_type=pl.DeviceIdType.MESH,
        )

    whole = jnp.concatenate([density[z] for z in range(cells)], axis=1)
    packed[...] = matmul(whole, pack_m[...]).astype(bf16)
    to_left = remote(packed, from_right, tile_send.at[0], tile_recv.at[1], {"tile": t - 1})
    to_right = remote(packed, from_left, tile_send.at[1], tile_recv.at[0], {"tile": t + 1})

    pl.semaphore_wait(
        barrier, slabs - 1 + (t > 0).astype(jnp.int32) + (t < tiles - 1).astype(jnp.int32)
    )

    to_below = remote(density, from_high, depth_send.at[0], depth_recv.at[1], {"depth": d - 1})
    to_above = remote(density, from_low, depth_send.at[1], depth_recv.at[0], {"depth": d + 1})

    @pl.when(t > 0)
    def _():
        to_left.start()

    @pl.when(t < tiles - 1)
    def _():
        to_right.start()

    @pl.when(d > 0)
    def _():
        to_below.start()

    @pl.when(d < slabs - 1)
    def _():
        to_above.start()

    @pl.when(t == 0)
    def _():
        from_left[...] = jnp.zeros_like(from_left)

    @pl.when(t == tiles - 1)
    def _():
        from_right[...] = jnp.zeros_like(from_right)

    @pl.when(d == 0)
    def _():
        from_low[...] = jnp.zeros_like(from_low)
        edges_low[...] = jnp.zeros_like(edges_low)

    @pl.when(d == slabs - 1)
    def _():
        from_high[...] = jnp.zeros_like(from_high)
        edges_high[...] = jnp.zeros_like(edges_high)

    pixel = lax.broadcasted_iota(jnp.int32, (rows, rows), 0).astype(jnp.float32)
    cell = lax.broadcasted_iota(jnp.int32, (rows, rows), 1).astype(jnp.float32)
    for v in range(views):
        where_at = zoom[v] * pixel + shift[v]
        table[v * rows : (v + 1) * rows] = jnp.maximum(0.0, 1.0 - jnp.abs(where_at - cell)).astype(bf16)

    def resample(source):
        for z in range(0, cells, 2):
            pair = matmul(table[...], jnp.concatenate([source[z], source[z + 1]], axis=1))
            sampled[z] = pair[:, :width]
            sampled[z + 1] = pair[:, width:]

    resample(density)
    for fetch in fetches[2:]:
        fetch.wait()

    @pl.when(t > 0)
    def _():
        to_left.wait_send()
        to_right.wait_recv()

    @pl.when(t < tiles - 1)
    def _():
        to_right.wait_send()
        to_left.wait_recv()

    lane = lax.broadcasted_iota(jnp.int32, (rows, width), 1)
    edges[...] = jnp.where(
        lane < cells * RADIUS, from_right[...].astype(jnp.float32), from_left[...].astype(jnp.float32)
    ).astype(bf16)

    def blur_plane(block, sides, out):
        inner = matmul(block[...].reshape(cells * rows, width), width_m[...])
        outer = matmul(sides[...], halo_m[...])
        along_width = jnp.concatenate(
            [inner[z * rows : (z + 1) * rows] + outer[:, z * width : (z + 1) * width] for z in range(cells)],
            axis=1,
        ).astype(bf16)
        flat = matmul(height_m[...], along_width).astype(bf16)
        for z in range(cells):
            out[z] = flat[:, z * width : (z + 1) * width]

    edges_below = remote(edges, edges_high, edge_send.at[0], edge_recv.at[1], {"depth": d - 1})
    edges_above = remote(edges, edges_low, edge_send.at[1], edge_recv.at[0], {"depth": d + 1})

    @pl.when(d > 0)
    def _():
        edges_below.start()

    @pl.when(d < slabs - 1)
    def _():
        edges_above.start()

    blur_plane(density, edges, plane)

    chunk = min(CHUNK, group_rows)
    per_group = group_rows // chunk
    extinction = -(EXTINCTION / (cells * slabs)) * LOG2E
    peak = basis - 1
    for v in range(views):
        coef = [
            [
                weights[v, c, k] * (math.exp(-0.5 * k * k) * (extinction if c == channels - 1 else 1.0))
                for k in range(basis)
            ]
            for c in range(channels)
        ]

        def transfer(i, carry, v=v, coef=coef):
            first = pl.multiple_of(i * chunk, chunk)
            passing = jnp.ones((chunk, width), jnp.float32)
            for z in range(cells):
                s = sampled[z, pl.ds(v * rows + first, chunk), :]
                fall = jnp.exp2((-0.5 * peak * peak * LOG2E) * (s * s))
                ratio = jnp.exp2((peak * LOG2E) * s)
                sums = []
                for c in range(channels):
                    total = coef[c][basis - 1] * ratio + coef[c][basis - 2]
                    for k in range(basis - 3, -1, -1):
                        total = total * ratio + coef[c][k]
                    sums.append(total)
                later = passing * jnp.exp2(fall * sums[-1])
                share = (passing - later) * fall
                for c in range(channels - 1):
                    lit[v, c, z, pl.ds(first, chunk), :] = share * sums[c]
                passing = later
            group = i // per_group
            inside = pl.multiple_of((i % per_group) * chunk, chunk)
            alpha[group, v, pl.ds(inside, chunk), :] = (1.0 - passing).astype(bf16)
            return carry

        lax.fori_loop(0, rows // chunk, transfer, 0)

    def peer_of(k):
        return lax.rem(d + k, slabs)

    def alpha_copy(k):
        return remote(alpha.at[peer_of(k)], recv_alpha.at[d], alpha_send.at[k], alpha_recv.at[d], {"depth": peer_of(k)})

    others = sorted(range(1, slabs), key=lambda k: abs(2 * k - slabs))
    for k in others:
        alpha_copy(k).start()
    recv_alpha[d] = alpha[d]

    @pl.when(d > 0)
    def _():
        to_below.wait_send()
        to_above.wait_recv()
        edges_below.wait_send()
        edges_above.wait_recv()

    @pl.when(d < slabs - 1)
    def _():
        to_above.wait_send()
        to_below.wait_recv()
        edges_above.wait_send()
        edges_below.wait_recv()

    blur_plane(from_low, edges_low, plane_low)
    blur_plane(from_high, edges_high, plane_high)
    gain = -OCCLUSION_GAIN * LOG2E / tap_total**3
    for g in range(0, rows, 2 * GROUP):
        def column(at):
            part = pl.ds(at, GROUP)
            return jnp.concatenate(
                [ref[:, part, :].reshape(cells * GROUP, width) for ref in (plane_low, plane, plane_high)], axis=0
            )

        both = matmul(depth_m[...], jnp.concatenate([column(g), column(g + GROUP)], axis=1))
        both = jnp.exp2(gain * both).astype(bf16)
        shade[:, g : g + GROUP, :] = both[:, :width].reshape(cells, GROUP, width)
        shade[:, g + GROUP : g + 2 * GROUP, :] = both[:, width:].reshape(cells, GROUP, width)
    resample(shade)

    def slab_copy(v, k):
        return remote(
            slab.at[v, k], recv[v].at[d], slab_send.at[v, k], slab_recv.at[v, d], {"depth": peer_of(k)}
        )

    for v in range(views):
        for k in others + [0]:
            start = pl.multiple_of(peer_of(k) * group_rows, group_rows)
            for i in range(per_group):
                colour = [jnp.zeros((chunk, width), jnp.float32)] * (channels - 1)
                for z in range(cells):
                    s = sampled[z, pl.ds(v * rows + start + i * chunk, chunk), :]
                    colour = [
                        colour[c] + lit[v, c, z, pl.ds(start + i * chunk, chunk), :] * s
                        for c in range(channels - 1)
                    ]
                for c in range(channels - 1):
                    tint = colour[c].astype(bf16)
                    if k:
                        slab[v, k, c, i * chunk : (i + 1) * chunk, :] = tint
                    else:
                        recv[v][d, c, i * chunk : (i + 1) * chunk, :] = tint
            if k:
                slab_copy(v, k).start()

    for k in others:
        peer = peer_of(k)
        alpha_copy(k).wait_send()
        remote(
            alpha.at[peer], recv_alpha.at[peer], alpha_send.at[k], alpha_recv.at[peer], {"depth": peer}
        ).wait_recv()
    for v in range(views):
        for k in others:
            peer = peer_of(k)
            slab_copy(v, k).wait_send()
            remote(
                slab.at[v, k], recv[v].at[peer], slab_send.at[v, k], slab_recv.at[v, peer], {"depth": peer}
            ).wait_recv()

        picture = jnp.zeros((channels - 1, group_rows, width), jnp.float32)
        cover = jnp.zeros((group_rows, width), jnp.float32)
        passing = jnp.ones((group_rows, width), jnp.float32)
        for q in range(slabs):
            slot = order[v, q]
            dense = recv_alpha[slot, v].astype(jnp.float32)
            picture = picture + passing[None] * recv[v][slot].astype(jnp.float32)
            cover = cover + passing * dense
            passing = passing * (1.0 - dense)
        image[v, : channels - 1] = picture
        image[v, channels - 1] = cover


def local(slabs, tiles, density, view_zoom, view_shift, tf_weights, perm_order):
    cells, rows, width = density.shape
    views, channels, _ = tf_weights.shape
    group_rows = rows // slabs
    matrices, tap_total = constants(cells, rows, width)
    vmem = pl.BlockSpec(memory_space=pltpu.VMEM)
    hbm = pl.BlockSpec(memory_space=pl.ANY)
    smem = pl.BlockSpec(memory_space=pltpu.SMEM)
    bf16 = jnp.bfloat16
    block = pltpu.VMEM((cells, rows, width), bf16)
    edge = pltpu.VMEM((rows, width), bf16)
    dma = pltpu.SemaphoreType.DMA
    return pl.pallas_call(
        functools.partial(kernel, slabs, tiles, tap_total),
        out_shape=jax.ShapeDtypeStruct((views, channels, group_rows, width), jnp.float32),
        in_specs=[hbm, smem, smem, smem, smem] + [hbm] * len(matrices),
        out_specs=vmem,
        scratch_shapes=[block]
        + [pltpu.VMEM(m.shape, bf16) for m in matrices]
        + [
            pltpu.VMEM((views * rows, rows), bf16),
            edge, edge, edge, edge, edge, edge,
            block, block, block, block, block,
            pltpu.VMEM((cells, views * rows, width), jnp.float32),
            pltpu.VMEM((views, channels - 1, cells, rows, width), jnp.float32),
            block,
            pltpu.VMEM((slabs, views, group_rows, width), bf16),
            pltpu.VMEM((views, slabs, channels - 1, group_rows, width), bf16),
            pltpu.VMEM((slabs, views, group_rows, width), bf16),
        ]
        + [pltpu.VMEM((slabs, channels - 1, group_rows, width), bf16)] * views
        + [dma((1 + len(matrices),)), dma((2,)), dma((2,)), dma((2,)), dma((2,)), dma((2,)), dma((2,))]
        + [dma((slabs,)), dma((slabs,))]
        + [dma((views, slabs)), dma((views, slabs))],
        compiler_params=pltpu.CompilerParams(
            collective_id=0, has_side_effects=True, vmem_limit_bytes=60 * 1024 * 1024
        ),
    )(density, view_zoom, view_shift, tf_weights, perm_order, *matrices)


def solution(mesh):
    placed = (P("depth", None, "tile"), P(), P(), P(), P())
    return jax.shard_map(
        functools.partial(local, mesh.shape["depth"], mesh.shape["tile"]),
        mesh=mesh, in_specs=placed, out_specs=P(None, None, "depth", "tile"), check_vma=False,
    )
```

```python
import functools
import math

import jax
import jax.numpy as jnp
import numpy as np
from jax import lax
from jax.experimental import pallas as pl
from jax.experimental.pallas import tpu as pltpu
from jax.sharding import PartitionSpec as P

RADIUS = 8
OCCLUSION_GAIN = 1.5
EXTINCTION = 0.5
LOG2E = math.log2(math.e)
GROUP = 16
CHUNK = 32


def rounded_taps():
    offsets = np.arange(-RADIUS, RADIUS + 1, dtype=np.float64)
    taps = np.exp(-offsets * offsets / 72.0)
    taps = (taps / taps.sum()).astype(jnp.bfloat16).astype(np.float64)
    return taps, float(taps.sum())


def band(out_count, in_count, shift, taps):
    offset = np.arange(in_count)[None, :] + shift - np.arange(out_count)[:, None]
    inside = np.abs(offset) <= RADIUS
    return np.where(inside, taps[np.clip(offset + RADIUS, 0, 2 * RADIUS)], 0.0)


def constants(cells, rows, width):
    taps, total = rounded_taps()
    pack = np.zeros((cells, width, width), np.float32)
    low = np.zeros((width, cells, width))
    high = np.zeros((width, cells, width))
    half = cells * RADIUS
    from_low = band(width, RADIUS, -RADIUS, taps).T
    from_high = band(width, RADIUS, width, taps).T
    for z in range(cells):
        for j in range(RADIUS):
            pack[z, j, z * RADIUS + j] = 1.0
            pack[z, width - RADIUS + j, half + z * RADIUS + j] = 1.0
        low[half + z * RADIUS : half + (z + 1) * RADIUS, z] = from_low
        high[z * RADIUS : (z + 1) * RADIUS, z] = from_high
    halo = (low + high).reshape(width, cells * width)
    depth = np.kron(band(cells, 3 * cells, -cells, taps), np.eye(GROUP))
    arrays = (
        pack.reshape(cells * width, width),
        band(width, width, 0, taps).T,
        halo,
        band(rows, rows, 0, taps),
        depth,
    )
    return [jnp.asarray(a.astype(jnp.bfloat16)) for a in arrays], total


def matmul(a, b):
    return jnp.dot(a, b, preferred_element_type=jnp.float32)


def kernel(
    slabs, tiles, tap_total,
    density_in, zoom, shift, weights, order, pack_in, width_in, halo_in, height_in, depth_in,
    image_out,
    density, pack_m, width_m, halo_m, height_m, depth_m,
    table, packed, from_left, from_right, edges, edges_low, edges_high,
    plane, plane_low, plane_high, from_low, from_high, sampled, lit, shade, alpha, slab, recv_alpha, image, *rest,
):
    views, channels, basis = weights.shape
    cells, rows, width = density_in.shape
    recv = rest[:views]
    fetch_sem, out_sem, tile_send, tile_recv, depth_send, depth_recv, edge_send, edge_recv, alpha_send, alpha_recv, slab_send, slab_recv = rest[views:]
    group_rows = rows // slabs
    d = lax.axis_index("depth")
    t = lax.axis_index("tile")
    bf16 = jnp.bfloat16

    barrier = pltpu.get_barrier_semaphore()

    def greet(peer):
        pl.semaphore_signal(barrier, inc=1, device_id=peer, device_id_type=pl.DeviceIdType.MESH)

    for j in range(slabs):
        @pl.when(j != d)
        def _():
            greet({"depth": j})

    @pl.when(t > 0)
    def _():
        greet({"tile": t - 1})

    @pl.when(t < tiles - 1)
    def _():
        greet({"tile": t + 1})

    sources = (density_in, pack_in, width_in, halo_in, height_in, depth_in)
    places = (density, pack_m, width_m, halo_m, height_m, depth_m)
    fetches = [
        pltpu.make_async_copy(src, dst, fetch_sem.at[i]) for i, (src, dst) in enumerate(zip(sources, places))
    ]
    for fetch in fetches:
        fetch.start()
    fetches[0].wait()
    fetches[1].wait()

    def remote(src, dst, send, recv_sem, peer):
        return pltpu.make_async_remote_copy(
            src_ref=src, dst_ref=dst, send_sem=send, recv_sem=recv_sem,
            device_id=peer, device_id_type=pl.DeviceIdType.MESH,
        )

    whole = jnp.concatenate([density[z] for z in range(cells)], axis=1)
    packed[...] = matmul(whole, pack_m[...]).astype(bf16)
    to_left = remote(packed, from_right, tile_send.at[0], tile_recv.at[1], {"tile": t - 1})
    to_right = remote(packed, from_left, tile_send.at[1], tile_recv.at[0], {"tile": t + 1})

    pl.semaphore_wait(
        barrier, slabs - 1 + (t > 0).astype(jnp.int32) + (t < tiles - 1).astype(jnp.int32)
    )

    half = cells // 2
    parts = [slice(0, half), slice(half, cells)]
    to_below = [
        remote(density.at[p], from_high.at[p], depth_send.at[0, i], depth_recv.at[1, i], {"depth": d - 1})
        for i, p in enumerate(parts)
    ]
    to_above = [
        remote(density.at[p], from_low.at[p], depth_send.at[1, i], depth_recv.at[0, i], {"depth": d + 1})
        for i, p in enumerate(parts)
    ]

    @pl.when(t > 0)
    def _():
        to_left.start()

    @pl.when(t < tiles - 1)
    def _():
        to_right.start()

    @pl.when(d > 0)
    def _():
        to_below[0].start()

    @pl.when(d < slabs - 1)
    def _():
        to_above[0].start()

    @pl.when(t == 0)
    def _():
        from_left[...] = jnp.zeros_like(from_left)

    @pl.when(t == tiles - 1)
    def _():
        from_right[...] = jnp.zeros_like(from_right)

    @pl.when(d == 0)
    def _():
        from_low[...] = jnp.zeros_like(from_low)
        edges_low[...] = jnp.zeros_like(edges_low)

    @pl.when(d == slabs - 1)
    def _():
        from_high[...] = jnp.zeros_like(from_high)
        edges_high[...] = jnp.zeros_like(edges_high)

    pixel = lax.broadcasted_iota(jnp.int32, (rows, rows), 0).astype(jnp.float32)
    cell = lax.broadcasted_iota(jnp.int32, (rows, rows), 1).astype(jnp.float32)
    for v in range(views):
        where_at = zoom[v] * pixel + shift[v]
        table[v * rows : (v + 1) * rows] = jnp.maximum(0.0, 1.0 - jnp.abs(where_at - cell)).astype(bf16)

    def resample(source):
        for z in range(0, cells, 2):
            pair = matmul(table[...], jnp.concatenate([source[z], source[z + 1]], axis=1))
            sampled[z] = pair[:, :width]
            sampled[z + 1] = pair[:, width:]

    resample(density)
    for fetch in fetches[2:]:
        fetch.wait()

    @pl.when(t > 0)
    def _():
        to_left.wait_send()
        to_right.wait_recv()

    @pl.when(t < tiles - 1)
    def _():
        to_right.wait_send()
        to_left.wait_recv()

    lane = lax.broadcasted_iota(jnp.int32, (rows, width), 1)
    edges[...] = jnp.where(
        lane < cells * RADIUS, from_right[...].astype(jnp.float32), from_left[...].astype(jnp.float32)
    ).astype(bf16)

    def blur_plane(block, sides, out, part):
        count = part.stop - part.start
        inner = matmul(block[part].reshape(count * rows, width), width_m[...])
        outer = matmul(sides[...], halo_m[:, part.start * width : part.stop * width])
        along_width = jnp.concatenate(
            [inner[z * rows : (z + 1) * rows] + outer[:, z * width : (z + 1) * width] for z in range(count)],
            axis=1,
        ).astype(bf16)
        flat = matmul(height_m[...], along_width).astype(bf16)
        for z in range(count):
            out[part.start + z] = flat[:, z * width : (z + 1) * width]

    edges_below = remote(edges, edges_high, edge_send.at[0], edge_recv.at[1], {"depth": d - 1})
    edges_above = remote(edges, edges_low, edge_send.at[1], edge_recv.at[0], {"depth": d + 1})

    @pl.when(d > 0)
    def _():
        edges_below.start()
        to_below[1].start()

    @pl.when(d < slabs - 1)
    def _():
        edges_above.start()
        to_above[1].start()

    blur_plane(density, edges, plane, slice(0, cells))

    chunk = min(CHUNK, group_rows)
    per_group = group_rows // chunk
    extinction = -(EXTINCTION / (cells * slabs)) * LOG2E
    peak = basis - 1
    for v in range(views):
        coef = [
            [
                weights[v, c, k] * (math.exp(-0.5 * k * k) * (extinction if c == channels - 1 else 1.0))
                for k in range(basis)
            ]
            for c in range(channels)
        ]

        def transfer(i, carry, v=v, coef=coef):
            first = pl.multiple_of(i * chunk, chunk)
            passing = jnp.ones((chunk, width), jnp.float32)
            for z in range(cells):
                s = sampled[z, pl.ds(v * rows + first, chunk), :]
                fall = jnp.exp2((-0.5 * peak * peak * LOG2E) * (s * s))
                ratio = jnp.exp2((peak * LOG2E) * s)
                sums = []
                for c in range(channels):
                    total = coef[c][basis - 1] * ratio + coef[c][basis - 2]
                    for k in range(basis - 3, -1, -1):
                        total = total * ratio + coef[c][k]
                    sums.append(total)
                later = passing * jnp.exp2(fall * sums[-1])
                share = (passing - later) * fall
                for c in range(channels - 1):
                    lit[v, c, z, pl.ds(first, chunk), :] = share * sums[c]
                passing = later
            group = i // per_group
            inside = pl.multiple_of((i % per_group) * chunk, chunk)
            alpha[group, v, pl.ds(inside, chunk), :] = (1.0 - passing).astype(bf16)
            return carry

        lax.fori_loop(0, rows // chunk, transfer, 0)

    def peer_of(k):
        return lax.rem(d + k, slabs)

    def alpha_copy(k):
        return remote(alpha.at[peer_of(k)], recv_alpha.at[d], alpha_send.at[k], alpha_recv.at[d], {"depth": peer_of(k)})

    others = sorted(range(1, slabs), key=lambda k: abs(2 * k - slabs))
    for k in others:
        alpha_copy(k).start()
    recv_alpha[d] = alpha[d]

    for i, part in enumerate(parts):
        @pl.when(d > 0)
        def _():
            to_below[i].wait_send()
            to_above[i].wait_recv()
            if i == 0:
                edges_below.wait_send()
                edges_above.wait_recv()

        @pl.when(d < slabs - 1)
        def _():
            to_above[i].wait_send()
            to_below[i].wait_recv()
            if i == 0:
                edges_above.wait_send()
                edges_below.wait_recv()

        blur_plane(from_low, edges_low, plane_low, part)
        blur_plane(from_high, edges_high, plane_high, part)

    gain = -OCCLUSION_GAIN * LOG2E / tap_total**3
    for g in range(0, rows, 2 * GROUP):
        def column(at):
            part = pl.ds(at, GROUP)
            return jnp.concatenate(
                [ref[:, part, :].reshape(cells * GROUP, width) for ref in (plane_low, plane, plane_high)], axis=0
            )

        both = matmul(depth_m[...], jnp.concatenate([column(g), column(g + GROUP)], axis=1))
        both = jnp.exp2(gain * both).astype(bf16)
        shade[:, g : g + GROUP, :] = both[:, :width].reshape(cells, GROUP, width)
        shade[:, g + GROUP : g + 2 * GROUP, :] = both[:, width:].reshape(cells, GROUP, width)
    resample(shade)

    def slab_copy(v, k):
        return remote(
            slab.at[v, k], recv[v].at[d], slab_send.at[v, k], slab_recv.at[v, d], {"depth": peer_of(k)}
        )

    for v in range(views):
        for k in others + [0]:
            start = pl.multiple_of(peer_of(k) * group_rows, group_rows)
            for i in range(per_group):
                colour = [jnp.zeros((chunk, width), jnp.float32)] * (channels - 1)
                for z in range(cells):
                    s = sampled[z, pl.ds(v * rows + start + i * chunk, chunk), :]
                    colour = [
                        colour[c] + lit[v, c, z, pl.ds(start + i * chunk, chunk), :] * s
                        for c in range(channels - 1)
                    ]
                for c in range(channels - 1):
                    tint = colour[c].astype(bf16)
                    if k:
                        slab[v, k, c, i * chunk : (i + 1) * chunk, :] = tint
                    else:
                        recv[v][d, c, i * chunk : (i + 1) * chunk, :] = tint
            if k:
                slab_copy(v, k).start()

    for k in others:
        peer = peer_of(k)
        alpha_copy(k).wait_send()
        remote(
            alpha.at[peer], recv_alpha.at[peer], alpha_send.at[k], alpha_recv.at[peer], {"depth": peer}
        ).wait_recv()
    for v in range(views):
        for k in others:
            peer = peer_of(k)
            slab_copy(v, k).wait_send()
            remote(
                slab.at[v, k], recv[v].at[peer], slab_send.at[v, k], slab_recv.at[v, peer], {"depth": peer}
            ).wait_recv()

        picture = jnp.zeros((channels - 1, group_rows, width), jnp.float32)
        cover = jnp.zeros((group_rows, width), jnp.float32)
        passing = jnp.ones((group_rows, width), jnp.float32)
        for q in range(slabs):
            slot = order[v, q]
            dense = recv_alpha[slot, v].astype(jnp.float32)
            picture = picture + passing[None] * recv[v][slot].astype(jnp.float32)
            cover = cover + passing * dense
            passing = passing * (1.0 - dense)
        image[v, : channels - 1] = picture
        image[v, channels - 1] = cover
        pltpu.make_async_copy(image.at[v], image_out.at[v], out_sem.at[v]).start()

    for v in range(views):
        pltpu.make_async_copy(image.at[v], image_out.at[v], out_sem.at[v]).wait()


def local(slabs, tiles, density, view_zoom, view_shift, tf_weights, perm_order):
    cells, rows, width = density.shape
    views, channels, _ = tf_weights.shape
    group_rows = rows // slabs
    matrices, tap_total = constants(cells, rows, width)
    hbm = pl.BlockSpec(memory_space=pl.ANY)
    smem = pl.BlockSpec(memory_space=pltpu.SMEM)
    bf16 = jnp.bfloat16
    block = pltpu.VMEM((cells, rows, width), bf16)
    edge = pltpu.VMEM((rows, width), bf16)
    dma = pltpu.SemaphoreType.DMA
    return pl.pallas_call(
        functools.partial(kernel, slabs, tiles, tap_total),
        out_shape=jax.ShapeDtypeStruct((views, channels, group_rows, width), jnp.float32),
        in_specs=[hbm, smem, smem, smem, smem] + [hbm] * len(matrices),
        out_specs=hbm,
        scratch_shapes=[block]
        + [pltpu.VMEM(m.shape, bf16) for m in matrices]
        + [
            pltpu.VMEM((views * rows, rows), bf16),
            edge, edge, edge, edge, edge, edge,
            block, block, block, block, block,
            pltpu.VMEM((cells, views * rows, width), jnp.float32),
            pltpu.VMEM((views, channels - 1, cells, rows, width), jnp.float32),
            block,
            pltpu.VMEM((slabs, views, group_rows, width), bf16),
            pltpu.VMEM((views, slabs, channels - 1, group_rows, width), bf16),
            pltpu.VMEM((slabs, views, group_rows, width), bf16),
            pltpu.VMEM((views, channels, group_rows, width), jnp.float32),
        ]
        + [pltpu.VMEM((slabs, channels - 1, group_rows, width), bf16)] * views
        + [dma((1 + len(matrices),)), dma((views,)), dma((2,)), dma((2,)), dma((2, 2)), dma((2, 2)), dma((2,)), dma((2,))]
        + [dma((slabs,)), dma((slabs,))]
        + [dma((views, slabs)), dma((views, slabs))],
        compiler_params=pltpu.CompilerParams(
            collective_id=0, has_side_effects=True, vmem_limit_bytes=60 * 1024 * 1024
        ),
    )(density, view_zoom, view_shift, tf_weights, perm_order, *matrices)


def solution(mesh):
    placed = (P("depth", None, "tile"), P(), P(), P(), P())
    return jax.shard_map(
        functools.partial(local, mesh.shape["depth"], mesh.shape["tile"]),
        mesh=mesh, in_specs=placed, out_specs=P(None, None, "depth", "tile"), check_vma=False,
    )
```

```python
import functools
import math

import jax
import jax.numpy as jnp
import numpy as np
from jax import lax
from jax.experimental import pallas as pl
from jax.experimental.pallas import tpu as pltpu
from jax.sharding import PartitionSpec as P

RADIUS = 8
OCCLUSION_GAIN = 1.5
EXTINCTION = 0.5
LOG2E = math.log2(math.e)
GROUP = 16
CHUNK = 32


def rounded_taps():
    offsets = np.arange(-RADIUS, RADIUS + 1, dtype=np.float64)
    taps = np.exp(-offsets * offsets / 72.0)
    taps = (taps / taps.sum()).astype(jnp.bfloat16).astype(np.float64)
    return taps, float(taps.sum())


def band(out_count, in_count, shift, taps):
    offset = np.arange(in_count)[None, :] + shift - np.arange(out_count)[:, None]
    inside = np.abs(offset) <= RADIUS
    return np.where(inside, taps[np.clip(offset + RADIUS, 0, 2 * RADIUS)], 0.0)


def constants(cells, rows, width):
    taps, total = rounded_taps()
    pack = np.zeros((cells, width, width), np.float32)
    low = np.zeros((width, cells, width))
    high = np.zeros((width, cells, width))
    half = cells * RADIUS
    from_low = band(width, RADIUS, -RADIUS, taps).T
    from_high = band(width, RADIUS, width, taps).T
    for z in range(cells):
        for j in range(RADIUS):
            pack[z, j, z * RADIUS + j] = 1.0
            pack[z, width - RADIUS + j, half + z * RADIUS + j] = 1.0
        low[half + z * RADIUS : half + (z + 1) * RADIUS, z] = from_low
        high[z * RADIUS : (z + 1) * RADIUS, z] = from_high
    halo = (low + high).reshape(width, cells * width)
    depth = np.kron(band(cells, 3 * cells, -cells, taps), np.eye(GROUP))
    arrays = (
        pack.reshape(cells * width, width),
        band(width, width, 0, taps).T,
        halo,
        band(rows, rows, 0, taps),
        depth,
    )
    return [jnp.asarray(a.astype(jnp.bfloat16)) for a in arrays], total


def matmul(a, b):
    return jnp.dot(a, b, preferred_element_type=jnp.float32)


def kernel(
    slabs, tiles, tap_total,
    density_in, zoom, shift, weights, order, pack_in, width_in, halo_in, height_in, depth_in,
    image_out,
    density, pack_m, width_m, halo_m, height_m, depth_m,
    table, packed, from_left, from_right, edges, edges_low, edges_high,
    plane, plane_low, plane_high, from_low, from_high, sampled, lit, shade, alpha, slab, recv_alpha, image, *rest,
):
    views, channels, basis = weights.shape
    cells, rows, width = density_in.shape
    recv = rest[:views]
    fetch_sem, out_sem, tile_send, tile_recv, depth_send, depth_recv, edge_send, edge_recv, alpha_send, alpha_recv, slab_send, slab_recv = rest[views:]
    group_rows = rows // slabs
    d = lax.axis_index("depth")
    t = lax.axis_index("tile")
    bf16 = jnp.bfloat16

    barrier = pltpu.get_barrier_semaphore()

    def greet(peer):
        pl.semaphore_signal(barrier, inc=1, device_id=peer, device_id_type=pl.DeviceIdType.MESH)

    for j in range(slabs):
        @pl.when(j != d)
        def _():
            greet({"depth": j})

    @pl.when(t > 0)
    def _():
        greet({"tile": t - 1})

    @pl.when(t < tiles - 1)
    def _():
        greet({"tile": t + 1})

    sources = (density_in, pack_in, width_in, halo_in, height_in, depth_in)
    places = (density, pack_m, width_m, halo_m, height_m, depth_m)
    fetches = [
        pltpu.make_async_copy(src, dst, fetch_sem.at[i]) for i, (src, dst) in enumerate(zip(sources, places))
    ]
    for fetch in fetches:
        fetch.start()

    def remote(src, dst, send, recv_sem, peer):
        return pltpu.make_async_remote_copy(
            src_ref=src, dst_ref=dst, send_sem=send, recv_sem=recv_sem,
            device_id=peer, device_id_type=pl.DeviceIdType.MESH,
        )

    to_left = remote(packed, from_right, tile_send.at[0], tile_recv.at[1], {"tile": t - 1})
    to_right = remote(packed, from_left, tile_send.at[1], tile_recv.at[0], {"tile": t + 1})

    pl.semaphore_wait(
        barrier, slabs - 1 + (t > 0).astype(jnp.int32) + (t < tiles - 1).astype(jnp.int32)
    )

    half = cells // 2
    parts = [slice(0, half), slice(half, cells)]
    to_below = [
        remote(density_in.at[p], from_high.at[p], depth_send.at[0, i], depth_recv.at[1, i], {"depth": d - 1})
        for i, p in enumerate(parts)
    ]
    to_above = [
        remote(density_in.at[p], from_low.at[p], depth_send.at[1, i], depth_recv.at[0, i], {"depth": d + 1})
        for i, p in enumerate(parts)
    ]

    @pl.when(d > 0)
    def _():
        to_below[0].start()

    @pl.when(d < slabs - 1)
    def _():
        to_above[0].start()

    fetches[0].wait()
    fetches[1].wait()
    whole = jnp.concatenate([density[z] for z in range(cells)], axis=1)
    packed[...] = matmul(whole, pack_m[...]).astype(bf16)
    @pl.when(t > 0)
    def _():
        to_left.start()

    @pl.when(t < tiles - 1)
    def _():
        to_right.start()

    @pl.when(t == 0)
    def _():
        from_left[...] = jnp.zeros_like(from_left)

    @pl.when(t == tiles - 1)
    def _():
        from_right[...] = jnp.zeros_like(from_right)

    @pl.when(d == 0)
    def _():
        from_low[...] = jnp.zeros_like(from_low)
        edges_low[...] = jnp.zeros_like(edges_low)

    @pl.when(d == slabs - 1)
    def _():
        from_high[...] = jnp.zeros_like(from_high)
        edges_high[...] = jnp.zeros_like(edges_high)

    pixel = lax.broadcasted_iota(jnp.int32, (rows, rows), 0).astype(jnp.float32)
    cell = lax.broadcasted_iota(jnp.int32, (rows, rows), 1).astype(jnp.float32)
    for v in range(views):
        where_at = zoom[v] * pixel + shift[v]
        table[v * rows : (v + 1) * rows] = jnp.maximum(0.0, 1.0 - jnp.abs(where_at - cell)).astype(bf16)

    def resample(source):
        for z in range(0, cells, 2):
            pair = matmul(table[...], jnp.concatenate([source[z], source[z + 1]], axis=1))
            sampled[z] = pair[:, :width]
            sampled[z + 1] = pair[:, width:]

    resample(density)
    for fetch in fetches[2:]:
        fetch.wait()

    @pl.when(t > 0)
    def _():
        to_left.wait_send()
        to_right.wait_recv()

    @pl.when(t < tiles - 1)
    def _():
        to_right.wait_send()
        to_left.wait_recv()

    lane = lax.broadcasted_iota(jnp.int32, (rows, width), 1)
    edges[...] = jnp.where(
        lane < cells * RADIUS, from_right[...].astype(jnp.float32), from_left[...].astype(jnp.float32)
    ).astype(bf16)

    def blur_plane(block, sides, out, part):
        count = part.stop - part.start
        inner = matmul(block[part].reshape(count * rows, width), width_m[...])
        outer = matmul(sides[...], halo_m[:, part.start * width : part.stop * width])
        along_width = jnp.concatenate(
            [inner[z * rows : (z + 1) * rows] + outer[:, z * width : (z + 1) * width] for z in range(count)],
            axis=1,
        ).astype(bf16)
        flat = matmul(height_m[...], along_width).astype(bf16)
        for z in range(count):
            out[part.start + z] = flat[:, z * width : (z + 1) * width]

    edges_below = remote(edges, edges_high, edge_send.at[0], edge_recv.at[1], {"depth": d - 1})
    edges_above = remote(edges, edges_low, edge_send.at[1], edge_recv.at[0], {"depth": d + 1})

    @pl.when(d > 0)
    def _():
        edges_below.start()
        to_below[1].start()

    @pl.when(d < slabs - 1)
    def _():
        edges_above.start()
        to_above[1].start()

    blur_plane(density, edges, plane, slice(0, cells))

    chunk = min(CHUNK, group_rows)
    per_group = group_rows // chunk
    extinction = -(EXTINCTION / (cells * slabs)) * LOG2E
    peak = basis - 1
    for v in range(views):
        coef = [
            [
                weights[v, c, k] * (math.exp(-0.5 * k * k) * (extinction if c == channels - 1 else 1.0))
                for k in range(basis)
            ]
            for c in range(channels)
        ]

        def transfer(i, carry, v=v, coef=coef):
            first = pl.multiple_of(i * chunk, chunk)
            passing = jnp.ones((chunk, width), jnp.float32)
            for z in range(cells):
                s = sampled[z, pl.ds(v * rows + first, chunk), :]
                fall = jnp.exp2((-0.5 * peak * peak * LOG2E) * (s * s))
                ratio = jnp.exp2((peak * LOG2E) * s)
                sums = []
                for c in range(channels):
                    total = coef[c][basis - 1] * ratio + coef[c][basis - 2]
                    for k in range(basis - 3, -1, -1):
                        total = total * ratio + coef[c][k]
                    sums.append(total)
                later = passing * jnp.exp2(fall * sums[-1])
                share = (passing - later) * fall
                for c in range(channels - 1):
                    lit[v, c, z, pl.ds(first, chunk), :] = share * sums[c]
                passing = later
            group = i // per_group
            inside = pl.multiple_of((i % per_group) * chunk, chunk)
            alpha[group, v, pl.ds(inside, chunk), :] = (1.0 - passing).astype(bf16)
            return carry

        lax.fori_loop(0, rows // chunk, transfer, 0)

    def peer_of(k):
        return lax.rem(d + k, slabs)

    def alpha_copy(k):
        return remote(alpha.at[peer_of(k)], recv_alpha.at[d], alpha_send.at[k], alpha_recv.at[d], {"depth": peer_of(k)})

    others = sorted(range(1, slabs), key=lambda k: abs(2 * k - slabs))
    for k in others:
        alpha_copy(k).start()
    recv_alpha[d] = alpha[d]

    for i, part in enumerate(parts):
        @pl.when(d > 0)
        def _():
            to_below[i].wait_send()
            to_above[i].wait_recv()
            if i == 0:
                edges_below.wait_send()
                edges_above.wait_recv()

        @pl.when(d < slabs - 1)
        def _():
            to_above[i].wait_send()
            to_below[i].wait_recv()
            if i == 0:
                edges_above.wait_send()
                edges_below.wait_recv()

        blur_plane(from_low, edges_low, plane_low, part)
        blur_plane(from_high, edges_high, plane_high, part)

    gain = -OCCLUSION_GAIN * LOG2E / tap_total**3
    for g in range(0, rows, 2 * GROUP):
        def column(at):
            part = pl.ds(at, GROUP)
            return jnp.concatenate(
                [ref[:, part, :].reshape(cells * GROUP, width) for ref in (plane_low, plane, plane_high)], axis=0
            )

        both = matmul(depth_m[...], jnp.concatenate([column(g), column(g + GROUP)], axis=1))
        both = jnp.exp2(gain * both).astype(bf16)
        shade[:, g : g + GROUP, :] = both[:, :width].reshape(cells, GROUP, width)
        shade[:, g + GROUP : g + 2 * GROUP, :] = both[:, width:].reshape(cells, GROUP, width)
    resample(shade)

    def slab_copy(v, k):
        return remote(
            slab.at[v, k], recv[v].at[d], slab_send.at[v, k], slab_recv.at[v, d], {"depth": peer_of(k)}
        )

    for v in range(views):
        for k in others + [0]:
            start = pl.multiple_of(peer_of(k) * group_rows, group_rows)
            for i in range(per_group):
                colour = [jnp.zeros((chunk, width), jnp.float32)] * (channels - 1)
                for z in range(cells):
                    s = sampled[z, pl.ds(v * rows + start + i * chunk, chunk), :]
                    colour = [
                        colour[c] + lit[v, c, z, pl.ds(start + i * chunk, chunk), :] * s
                        for c in range(channels - 1)
                    ]
                for c in range(channels - 1):
                    tint = colour[c].astype(bf16)
                    if k:
                        slab[v, k, c, i * chunk : (i + 1) * chunk, :] = tint
                    else:
                        recv[v][d, c, i * chunk : (i + 1) * chunk, :] = tint
            if k:
                slab_copy(v, k).start()

    for k in others:
        peer = peer_of(k)
        alpha_copy(k).wait_send()
        remote(
            alpha.at[peer], recv_alpha.at[peer], alpha_send.at[k], alpha_recv.at[peer], {"depth": peer}
        ).wait_recv()
    for v in range(views):
        for k in others:
            peer = peer_of(k)
            slab_copy(v, k).wait_send()
            remote(
                slab.at[v, k], recv[v].at[peer], slab_send.at[v, k], slab_recv.at[v, peer], {"depth": peer}
            ).wait_recv()

        picture = jnp.zeros((channels - 1, group_rows, width), jnp.float32)
        cover = jnp.zeros((group_rows, width), jnp.float32)
        passing = jnp.ones((group_rows, width), jnp.float32)
        for q in range(slabs):
            slot = order[v, q]
            dense = recv_alpha[slot, v].astype(jnp.float32)
            picture = picture + passing[None] * recv[v][slot].astype(jnp.float32)
            cover = cover + passing * dense
            passing = passing * (1.0 - dense)
        image[v, : channels - 1] = picture
        image[v, channels - 1] = cover
        pltpu.make_async_copy(image.at[v], image_out.at[v], out_sem.at[v]).start()

    for v in range(views):
        pltpu.make_async_copy(image.at[v], image_out.at[v], out_sem.at[v]).wait()


def local(slabs, tiles, density, view_zoom, view_shift, tf_weights, perm_order):
    cells, rows, width = density.shape
    views, channels, _ = tf_weights.shape
    group_rows = rows // slabs
    matrices, tap_total = constants(cells, rows, width)
    hbm = pl.BlockSpec(memory_space=pl.ANY)
    smem = pl.BlockSpec(memory_space=pltpu.SMEM)
    bf16 = jnp.bfloat16
    block = pltpu.VMEM((cells, rows, width), bf16)
    edge = pltpu.VMEM((rows, width), bf16)
    dma = pltpu.SemaphoreType.DMA
    return pl.pallas_call(
        functools.partial(kernel, slabs, tiles, tap_total),
        out_shape=jax.ShapeDtypeStruct((views, channels, group_rows, width), jnp.float32),
        in_specs=[hbm, smem, smem, smem, smem] + [hbm] * len(matrices),
        out_specs=hbm,
        scratch_shapes=[block]
        + [pltpu.VMEM(m.shape, bf16) for m in matrices]
        + [
            pltpu.VMEM((views * rows, rows), bf16),
            edge, edge, edge, edge, edge, edge,
            block, block, block, block, block,
            pltpu.VMEM((cells, views * rows, width), jnp.float32),
            pltpu.VMEM((views, channels - 1, cells, rows, width), jnp.float32),
            block,
            pltpu.VMEM((slabs, views, group_rows, width), bf16),
            pltpu.VMEM((views, slabs, channels - 1, group_rows, width), bf16),
            pltpu.VMEM((slabs, views, group_rows, width), bf16),
            pltpu.VMEM((views, channels, group_rows, width), jnp.float32),
        ]
        + [pltpu.VMEM((slabs, channels - 1, group_rows, width), bf16)] * views
        + [dma((1 + len(matrices),)), dma((views,)), dma((2,)), dma((2,)), dma((2, 2)), dma((2, 2)), dma((2,)), dma((2,))]
        + [dma((slabs,)), dma((slabs,))]
        + [dma((views, slabs)), dma((views, slabs))],
        compiler_params=pltpu.CompilerParams(
            collective_id=0, has_side_effects=True, vmem_limit_bytes=60 * 1024 * 1024
        ),
    )(density, view_zoom, view_shift, tf_weights, perm_order, *matrices)


def solution(mesh):
    placed = (P("depth", None, "tile"), P(), P(), P(), P())
    return jax.shard_map(
        functools.partial(local, mesh.shape["depth"], mesh.shape["tile"]),
        mesh=mesh, in_specs=placed, out_specs=P(None, None, "depth", "tile"), check_vma=False,
    )
```

```python
import functools
import math

import jax
import jax.numpy as jnp
import numpy as np
from jax import lax
from jax.experimental import pallas as pl
from jax.experimental.pallas import tpu as pltpu
from jax.sharding import PartitionSpec as P

RADIUS = 8
OCCLUSION_GAIN = 1.5
EXTINCTION = 0.5
LOG2E = math.log2(math.e)
GROUP = 16
CHUNK = 32


def rounded_taps():
    offsets = np.arange(-RADIUS, RADIUS + 1, dtype=np.float64)
    taps = np.exp(-offsets * offsets / 72.0)
    taps = (taps / taps.sum()).astype(jnp.bfloat16).astype(np.float64)
    return taps, float(taps.sum())


def band(out_count, in_count, shift, taps):
    offset = np.arange(in_count)[None, :] + shift - np.arange(out_count)[:, None]
    inside = np.abs(offset) <= RADIUS
    return np.where(inside, taps[np.clip(offset + RADIUS, 0, 2 * RADIUS)], 0.0)


def constants(cells, rows, width):
    taps, total = rounded_taps()
    pack = np.zeros((cells, width, width), np.float32)
    low = np.zeros((width, cells, width))
    high = np.zeros((width, cells, width))
    half = cells * RADIUS
    from_low = band(width, RADIUS, -RADIUS, taps).T
    from_high = band(width, RADIUS, width, taps).T
    for z in range(cells):
        for j in range(RADIUS):
            pack[z, j, z * RADIUS + j] = 1.0
            pack[z, width - RADIUS + j, half + z * RADIUS + j] = 1.0
        low[half + z * RADIUS : half + (z + 1) * RADIUS, z] = from_low
        high[z * RADIUS : (z + 1) * RADIUS, z] = from_high
    halo = (low + high).reshape(width, cells * width)
    depth = np.kron(band(cells, 3 * cells, -cells, taps), np.eye(GROUP))
    arrays = (
        pack.reshape(cells * width, width),
        band(width, width, 0, taps).T,
        halo,
        band(rows, rows, 0, taps),
        depth,
    )
    return [jnp.asarray(a.astype(jnp.bfloat16)) for a in arrays], total


def matmul(a, b):
    return jnp.dot(a, b, preferred_element_type=jnp.float32)


def kernel(
    slabs, tiles, tap_total,
    density_in, zoom, shift, weights, order, pack_in, width_in, halo_in, height_in, depth_in,
    image_out,
    density, pack_m, width_m, halo_m, height_m, depth_m,
    table, packed, from_left, from_right, edges, edges_low, edges_high,
    plane, plane_low, plane_high, from_low, from_high, sampled, lit, shade, alpha, slab, recv_alpha, image, *rest,
):
    views, channels, basis = weights.shape
    cells, rows, width = density_in.shape
    recv = rest[:views]
    fetch_sem, out_sem, tile_send, tile_recv, depth_send, depth_recv, edge_send, edge_recv, alpha_send, alpha_recv, slab_send, slab_recv = rest[views:]
    group_rows = rows // slabs
    d = lax.axis_index("depth")
    t = lax.axis_index("tile")
    bf16 = jnp.bfloat16

    barrier = pltpu.get_barrier_semaphore()

    def greet(peer):
        pl.semaphore_signal(barrier, inc=1, device_id=peer, device_id_type=pl.DeviceIdType.MESH)

    for j in range(slabs):
        @pl.when(j != d)
        def _():
            greet({"depth": j})

    @pl.when(t > 0)
    def _():
        greet({"tile": t - 1})

    @pl.when(t < tiles - 1)
    def _():
        greet({"tile": t + 1})

    sources = (density_in, pack_in, width_in, halo_in, height_in, depth_in)
    places = (density, pack_m, width_m, halo_m, height_m, depth_m)
    fetches = [
        pltpu.make_async_copy(src, dst, fetch_sem.at[i]) for i, (src, dst) in enumerate(zip(sources, places))
    ]
    for fetch in fetches:
        fetch.start()
    fetches[0].wait()
    fetches[1].wait()

    def remote(src, dst, send, recv_sem, peer):
        return pltpu.make_async_remote_copy(
            src_ref=src, dst_ref=dst, send_sem=send, recv_sem=recv_sem,
            device_id=peer, device_id_type=pl.DeviceIdType.MESH,
        )

    whole = jnp.concatenate([density[z] for z in range(cells)], axis=1)
    packed[...] = matmul(whole, pack_m[...]).astype(bf16)
    to_left = remote(packed, from_right, tile_send.at[0], tile_recv.at[1], {"tile": t - 1})
    to_right = remote(packed, from_left, tile_send.at[1], tile_recv.at[0], {"tile": t + 1})

    pl.semaphore_wait(
        barrier, slabs - 1 + (t > 0).astype(jnp.int32) + (t < tiles - 1).astype(jnp.int32)
    )

    half = cells // 2
    parts = [slice(0, half), slice(half, cells)]
    to_below = [
        remote(density.at[p], from_high.at[p], depth_send.at[0, i], depth_recv.at[1, i], {"depth": d - 1})
        for i, p in enumerate(parts)
    ]
    to_above = [
        remote(density.at[p], from_low.at[p], depth_send.at[1, i], depth_recv.at[0, i], {"depth": d + 1})
        for i, p in enumerate(parts)
    ]

    @pl.when(t > 0)
    def _():
        to_left.start()

    @pl.when(t < tiles - 1)
    def _():
        to_right.start()

    @pl.when(d > 0)
    def _():
        to_below[0].start()

    @pl.when(d < slabs - 1)
    def _():
        to_above[0].start()

    @pl.when(t == 0)
    def _():
        from_left[...] = jnp.zeros_like(from_left)

    @pl.when(t == tiles - 1)
    def _():
        from_right[...] = jnp.zeros_like(from_right)

    @pl.when(d == 0)
    def _():
        from_low[...] = jnp.zeros_like(from_low)
        edges_low[...] = jnp.zeros_like(edges_low)

    @pl.when(d == slabs - 1)
    def _():
        from_high[...] = jnp.zeros_like(from_high)
        edges_high[...] = jnp.zeros_like(edges_high)

    pixel = lax.broadcasted_iota(jnp.int32, (rows, rows), 0).astype(jnp.float32)
    cell = lax.broadcasted_iota(jnp.int32, (rows, rows), 1).astype(jnp.float32)
    for v in range(views):
        where_at = zoom[v] * pixel + shift[v]
        table[v * rows : (v + 1) * rows] = jnp.maximum(0.0, 1.0 - jnp.abs(where_at - cell)).astype(bf16)

    def resample(source, v):
        at = slice(v * rows, (v + 1) * rows)
        for z in range(0, cells, 2):
            pair = matmul(table[at], jnp.concatenate([source[z], source[z + 1]], axis=1))
            sampled[z, at] = pair[:, :width]
            sampled[z + 1, at] = pair[:, width:]

    for v in range(views):
        resample(density, v)
    for fetch in fetches[2:]:
        fetch.wait()

    @pl.when(t > 0)
    def _():
        to_left.wait_send()
        to_right.wait_recv()

    @pl.when(t < tiles - 1)
    def _():
        to_right.wait_send()
        to_left.wait_recv()

    lane = lax.broadcasted_iota(jnp.int32, (rows, width), 1)
    edges[...] = jnp.where(
        lane < cells * RADIUS, from_right[...].astype(jnp.float32), from_left[...].astype(jnp.float32)
    ).astype(bf16)

    def blur_plane(block, sides, out, part):
        count = part.stop - part.start
        inner = matmul(block[part].reshape(count * rows, width), width_m[...])
        outer = matmul(sides[...], halo_m[:, part.start * width : part.stop * width])
        along_width = jnp.concatenate(
            [inner[z * rows : (z + 1) * rows] + outer[:, z * width : (z + 1) * width] for z in range(count)],
            axis=1,
        ).astype(bf16)
        flat = matmul(height_m[...], along_width).astype(bf16)
        for z in range(count):
            out[part.start + z] = flat[:, z * width : (z + 1) * width]

    edges_below = remote(edges, edges_high, edge_send.at[0], edge_recv.at[1], {"depth": d - 1})
    edges_above = remote(edges, edges_low, edge_send.at[1], edge_recv.at[0], {"depth": d + 1})

    @pl.when(d > 0)
    def _():
        edges_below.start()
        to_below[1].start()

    @pl.when(d < slabs - 1)
    def _():
        edges_above.start()
        to_above[1].start()

    blur_plane(density, edges, plane, slice(0, cells))

    chunk = min(CHUNK, group_rows)
    per_group = group_rows // chunk
    extinction = -(EXTINCTION / (cells * slabs)) * LOG2E
    peak = basis - 1
    for v in range(views):
        coef = [
            [
                weights[v, c, k] * (math.exp(-0.5 * k * k) * (extinction if c == channels - 1 else 1.0))
                for k in range(basis)
            ]
            for c in range(channels)
        ]

        def transfer(i, carry, v=v, coef=coef):
            first = pl.multiple_of(i * chunk, chunk)
            passing = jnp.ones((chunk, width), jnp.float32)
            for z in range(cells):
                s = sampled[z, pl.ds(v * rows + first, chunk), :]
                fall = jnp.exp2((-0.5 * peak * peak * LOG2E) * (s * s))
                ratio = jnp.exp2((peak * LOG2E) * s)
                sums = []
                for c in range(channels):
                    total = coef[c][basis - 1] * ratio + coef[c][basis - 2]
                    for k in range(basis - 3, -1, -1):
                        total = total * ratio + coef[c][k]
                    sums.append(total)
                later = passing * jnp.exp2(fall * sums[-1])
                share = (passing - later) * fall
                for c in range(channels - 1):
                    lit[v, c, z, pl.ds(first, chunk), :] = share * sums[c]
                passing = later
            group = i // per_group
            inside = pl.multiple_of((i % per_group) * chunk, chunk)
            alpha[group, v, pl.ds(inside, chunk), :] = (1.0 - passing).astype(bf16)
            return carry

        lax.fori_loop(0, rows // chunk, transfer, 0)

    def peer_of(k):
        return lax.rem(d + k, slabs)

    def alpha_copy(k):
        return remote(alpha.at[peer_of(k)], recv_alpha.at[d], alpha_send.at[k], alpha_recv.at[d], {"depth": peer_of(k)})

    others = sorted(range(1, slabs), key=lambda k: abs(2 * k - slabs))
    for k in others:
        alpha_copy(k).start()
    recv_alpha[d] = alpha[d]

    for i, part in enumerate(parts):
        @pl.when(d > 0)
        def _():
            to_below[i].wait_send()
            to_above[i].wait_recv()
            if i == 0:
                edges_below.wait_send()
                edges_above.wait_recv()

        @pl.when(d < slabs - 1)
        def _():
            to_above[i].wait_send()
            to_below[i].wait_recv()
            if i == 0:
                edges_above.wait_send()
                edges_below.wait_recv()

        blur_plane(from_low, edges_low, plane_low, part)
        blur_plane(from_high, edges_high, plane_high, part)

    gain = -OCCLUSION_GAIN * LOG2E / tap_total**3
    for g in range(0, rows, 2 * GROUP):
        def column(at):
            part = pl.ds(at, GROUP)
            return jnp.concatenate(
                [ref[:, part, :].reshape(cells * GROUP, width) for ref in (plane_low, plane, plane_high)], axis=0
            )

        both = matmul(depth_m[...], jnp.concatenate([column(g), column(g + GROUP)], axis=1))
        both = jnp.exp2(gain * both).astype(bf16)
        shade[:, g : g + GROUP, :] = both[:, :width].reshape(cells, GROUP, width)
        shade[:, g + GROUP : g + 2 * GROUP, :] = both[:, width:].reshape(cells, GROUP, width)

    def slab_copy(v, k):
        return remote(
            slab.at[v, k], recv[v].at[d], slab_send.at[v, k], slab_recv.at[v, d], {"depth": peer_of(k)}
        )

    for v in range(views):
        resample(shade, v)
        for k in others + [0]:
            start = pl.multiple_of(peer_of(k) * group_rows, group_rows)
            for i in range(per_group):
                colour = [jnp.zeros((chunk, width), jnp.float32)] * (channels - 1)
                for z in range(cells):
                    s = sampled[z, pl.ds(v * rows + start + i * chunk, chunk), :]
                    colour = [
                        colour[c] + lit[v, c, z, pl.ds(start + i * chunk, chunk), :] * s
                        for c in range(channels - 1)
                    ]
                for c in range(channels - 1):
                    tint = colour[c].astype(bf16)
                    if k:
                        slab[v, k, c, i * chunk : (i + 1) * chunk, :] = tint
                    else:
                        recv[v][d, c, i * chunk : (i + 1) * chunk, :] = tint
            if k:
                slab_copy(v, k).start()

    for k in others:
        peer = peer_of(k)
        alpha_copy(k).wait_send()
        remote(
            alpha.at[peer], recv_alpha.at[peer], alpha_send.at[k], alpha_recv.at[peer], {"depth": peer}
        ).wait_recv()
    for v in range(views):
        for k in others:
            peer = peer_of(k)
            slab_copy(v, k).wait_send()
            remote(
                slab.at[v, k], recv[v].at[peer], slab_send.at[v, k], slab_recv.at[v, peer], {"depth": peer}
            ).wait_recv()

        picture = jnp.zeros((channels - 1, group_rows, width), jnp.float32)
        cover = jnp.zeros((group_rows, width), jnp.float32)
        passing = jnp.ones((group_rows, width), jnp.float32)
        for q in range(slabs):
            slot = order[v, q]
            dense = recv_alpha[slot, v].astype(jnp.float32)
            picture = picture + passing[None] * recv[v][slot].astype(jnp.float32)
            cover = cover + passing * dense
            passing = passing * (1.0 - dense)
        image[v, : channels - 1] = picture
        image[v, channels - 1] = cover
        pltpu.make_async_copy(image.at[v], image_out.at[v], out_sem.at[v]).start()

    for v in range(views):
        pltpu.make_async_copy(image.at[v], image_out.at[v], out_sem.at[v]).wait()


def local(slabs, tiles, density, view_zoom, view_shift, tf_weights, perm_order):
    cells, rows, width = density.shape
    views, channels, _ = tf_weights.shape
    group_rows = rows // slabs
    matrices, tap_total = constants(cells, rows, width)
    hbm = pl.BlockSpec(memory_space=pl.ANY)
    smem = pl.BlockSpec(memory_space=pltpu.SMEM)
    bf16 = jnp.bfloat16
    block = pltpu.VMEM((cells, rows, width), bf16)
    edge = pltpu.VMEM((rows, width), bf16)
    dma = pltpu.SemaphoreType.DMA
    return pl.pallas_call(
        functools.partial(kernel, slabs, tiles, tap_total),
        out_shape=jax.ShapeDtypeStruct((views, channels, group_rows, width), jnp.float32),
        in_specs=[hbm, smem, smem, smem, smem] + [hbm] * len(matrices),
        out_specs=hbm,
        scratch_shapes=[block]
        + [pltpu.VMEM(m.shape, bf16) for m in matrices]
        + [
            pltpu.VMEM((views * rows, rows), bf16),
            edge, edge, edge, edge, edge, edge,
            block, block, block, block, block,
            pltpu.VMEM((cells, views * rows, width), jnp.float32),
            pltpu.VMEM((views, channels - 1, cells, rows, width), jnp.float32),
            block,
            pltpu.VMEM((slabs, views, group_rows, width), bf16),
            pltpu.VMEM((views, slabs, channels - 1, group_rows, width), bf16),
            pltpu.VMEM((slabs, views, group_rows, width), bf16),
            pltpu.VMEM((views, channels, group_rows, width), jnp.float32),
        ]
        + [pltpu.VMEM((slabs, channels - 1, group_rows, width), bf16)] * views
        + [dma((1 + len(matrices),)), dma((views,)), dma((2,)), dma((2,)), dma((2, 2)), dma((2, 2)), dma((2,)), dma((2,))]
        + [dma((slabs,)), dma((slabs,))]
        + [dma((views, slabs)), dma((views, slabs))],
        compiler_params=pltpu.CompilerParams(
            collective_id=0, has_side_effects=True, vmem_limit_bytes=60 * 1024 * 1024
        ),
    )(density, view_zoom, view_shift, tf_weights, perm_order, *matrices)


def solution(mesh):
    placed = (P("depth", None, "tile"), P(), P(), P(), P())
    return jax.shard_map(
        functools.partial(local, mesh.shape["depth"], mesh.shape["tile"]),
        mesh=mesh, in_specs=placed, out_specs=P(None, None, "depth", "tile"), check_vma=False,
    )
```
